32 devices in a mesh: study: 2 (over y), branch: 4 (over z), scen: 2 (over x), bus: 2 (over core).
Axes of the slice: x: 2, y: 2, z: 4, core: 2. Of those that a mesh axis runs over, the one named last changes fastest.
Arguments:
- ptdf: bfloat16 [1024, 4096], P(None, ('branch', 'bus')), may hold values from -0.21875 to 0.21875
- base_flow: bfloat16 [8, 2, 32, 4096], P('study', 'scen', None, ('branch', 'bus')), parts along dimension 0, may hold values from -6 to 6
- rate_class: int32 [4096], P(('branch', 'bus')), may hold values from 0 to 15
- class_limit: float32 [16], replicated, may hold values from 0.6 to 2
- site_block: int32 [8, 2, 2, 3], P('study', 'scen'), parts along dimension 0, may hold values from 0 to 3, as said below
- profile: bfloat16 [8, 2, 2, 32, 384], P(('study', 'branch'), 'scen', 'bus'), parts along dimension 0, may hold values from 0.099609375 to 1
- size_init: float32 [8, 2, 2, 384], P(('study', 'branch'), 'scen', 'bus'), parts along dimension 0, may hold values from 0.5 to 1.5
Outputs:
- size_final: float32 [8, 2, 2, 384], P(('study', 'branch'), 'scen', 'bus'), parts along dimension 0
- flows_last: bfloat16 [8, 2, 32, 4096], P('study', 'scen', None, ('branch', 'bus')), parts along dimension 0
The draws below stay inside these ranges and needn't reach their ends.
There are 2 independent parts, one for each index of `study`. The reference program is written for one: setup_inputs(seed, part) draws one part's arguments, and reference() takes and returns one part's arrays. A program takes and returns all parts, laid end to end along the dimension named above; an argument that names none is the same for every part. Nothing has to cross between parts.
Inputs may be any that keep to these rules, and one draw needn't show every extreme that they name: `site_block`: the 3 block numbers of one half of one batch's site list are distinct.
All inputs are finite; a program needn't handle non-finite values.
Results may differ from the reference program's by a relative error of at most 0.017.
Values may be sent and summed in bfloat16 or wider, within the bound.
A program may use at most 64 MiB of HBM per device.

```python
import math
import jax
import jax.numpy as jnp
from jax import lax

POOL = 1024
KB = 3
SCEN = 32
CLASSES = 16
OWNERS = 4
GROUPS = 2
BRANCHES = 4096
SITES = 384
HALF_BLK = 4


def draw_site_block(key, part):
    total_rows = OWNERS * GROUPS * 2
    subkeys = jax.random.split(jax.random.fold_in(key, 7), total_rows)

    def shuffled(single_key):
        return jax.random.permutation(single_key, HALF_BLK)
    orders = jax.vmap(shuffled)(subkeys)
    return orders[:, :KB].reshape(OWNERS, GROUPS, 2, KB).astype(jnp.int32)


def plant(entries, stream_key, least, top_value):
    place = [jax.random.randint(jax.random.fold_in(stream_key, axis), (), 0, length) for axis, length in enumerate(entries.shape)]
    main_axis = entries.shape.index(max(entries.shape))
    beside = place[:main_axis] + [(place[main_axis] + 1) % entries.shape[main_axis]] + place[main_axis + 1:]
    return entries.at[tuple(place)].set(least).at[tuple(beside)].set(top_value)


def block_scale(rng, extent, shards, smallest, largest):
    def one(position, shards_of):
        steps = jax.random.uniform(jax.random.fold_in(jax.random.fold_in(rng, 6), position), (shards_of,), jnp.float32, smallest / len(shards), largest / len(shards))
        return jnp.repeat(jnp.exp(steps), extent[position] // shards_of).reshape((-1,) + (1,) * (len(extent) - position - 1))

    gain = one(*shards[0])
    for cut in shards[1:]:
        gain = gain * one(*cut)
    return gain


def gaussian(rng, extent, deviation, most, pieces=(), held_as=jnp.bfloat16):
    gain = block_scale(rng, extent, pieces, -0.22, 0.18) if pieces else 1.0
    array = jax.random.normal(rng, extent, jnp.float32) * deviation * gain
    return jnp.minimum(jnp.maximum(array, -most), most).astype(held_as)


def setup_inputs(seed: int = 0, part: int = 0) -> dict:
    streams_of = jax.random.split(jax.random.key(seed), 8)
    own_keys = jax.random.split(jax.random.fold_in(streams_of[7], part), 8)
    return {
        "ptdf": gaussian(streams_of[0], (POOL, BRANCHES), (2 * SITES) ** -0.5, 0.21875, ((1, 8),)),
        "base_flow": gaussian(own_keys[1], (OWNERS, GROUPS, SCEN, BRANCHES), 1.0, 6.0, ((1, 2), (3, 8))),
        "rate_class": plant(jax.random.randint(streams_of[2], (BRANCHES,), 0, CLASSES), jax.random.fold_in(streams_of[2], 1), 0, CLASSES - 1).astype(jnp.int32),
        "class_limit": jnp.clip(jnp.exp(jax.random.uniform(streams_of[3], (CLASSES,), jnp.float32, math.log(0.6), math.log(2.0))), 0.6, 2.0),
        "site_block": draw_site_block(jax.random.fold_in(jax.random.fold_in(streams_of[7], part), 71), part),
        "profile": jnp.clip(0.099609375 + 0.9003906 * jax.random.uniform(own_keys[5], (OWNERS, GROUPS, 2, SCEN, SITES), jnp.float32) ** block_scale(own_keys[5], (OWNERS, GROUPS, 2, SCEN, SITES), ((0, 4), (1, 2), (2, 2)), -0.2, 0.2), 0.099609375, 1.0).astype(jnp.bfloat16),
        "size_init": jnp.clip(0.5 + 1.0 * jax.random.uniform(own_keys[6], (OWNERS, GROUPS, 2, SITES), jnp.float32) ** block_scale(own_keys[6], (OWNERS, GROUPS, 2, SITES), ((0, 4), (1, 2), (2, 2)), -0.2, 0.2), 0.5, 1.5),
    }


step_length = 3.0


def reference(ptdf, base_flow, rate_class, class_limit, site_block, profile, size_init):
    classes = jnp.arange(class_limit.shape[0], dtype=jnp.int32)
    rating = jnp.sum(jnp.where(rate_class[:, None] == classes[None, :], class_limit[None, :], 0.0), axis=1)
    owners = base_flow.shape[0]
    groups = base_flow.shape[1]
    scen_count = base_flow.shape[2]
    branch_count = base_flow.shape[3]
    half_pool = ptdf.shape[0] // 2
    site_count = profile.shape[-1]
    lane_index = jnp.arange(128, dtype=jnp.int32)
    halves = jnp.arange(2, dtype=jnp.int32) * half_pool
    columns = halves[None, None, :, None, None] + site_block[..., None] * 128 + lane_index[None, None, None, None, :]
    columns = columns.reshape(owners * groups, 2 * site_count).astype(jnp.int32)
    base_all = base_flow.reshape(owners * groups, scen_count, branch_count)
    profile_all = profile.reshape(owners * groups, 2, scen_count, site_count)
    sizes_all = size_init.reshape(owners * groups, 2 * site_count)

    def one_batch(batch_items):
        chosen, base_rows, profile_rows, sizes_flat = batch_items
        ptdf_block = jnp.take(ptdf, chosen, axis=0)
        profile_flat = jnp.concatenate([profile_rows[0], profile_rows[1]], axis=1)
        flow_now = jnp.zeros((scen_count, branch_count), jnp.float32)
        for sweep_index in range(2):
            injected = (sizes_flat[None, :] * profile_flat.astype(jnp.float32)).astype(jnp.bfloat16)
            flow_now = base_rows.astype(jnp.float32) + jnp.dot(injected, ptdf_block, preferred_element_type=jnp.float32)
            loading = flow_now / rating[None, :]
            adjoint = (jax.nn.sigmoid(loading * loading - 1.0) * 2.0 * loading / rating[None, :]).astype(jnp.bfloat16)
            sensitivity = lax.dot_general(adjoint, ptdf_block, (((1,), (1,)), ((), ())), preferred_element_type=jnp.float32)
            gradient = jnp.mean(profile_flat.astype(jnp.float32) * sensitivity, axis=0)
            sizes_flat = sizes_flat + step_length * (1.0 - gradient)
        return sizes_flat, flow_now.astype(jnp.bfloat16)

    final_sizes, last_flows = lax.map(one_batch, (columns, base_all, profile_all, sizes_all))
    return final_sizes.reshape(size_init.shape), last_flows.reshape(base_flow.shape)
```

```python
import functools
import jax
import jax.numpy as jnp
from jax import lax
from jax.experimental import pallas as pl
from jax.experimental.pallas import tpu as pltpu
from jax.sharding import PartitionSpec as P

step_length = 3.0
MESH = pl.DeviceIdType.MESH
FAR = 3


def kernel(
    n_branch, n_bus,
    ptdf_hbm, base_hbm, class_hbm, limit_hbm, block_hbm, profile_hbm, size_hbm,
    size_out, flow_out,
    limit_ref, block_ref, ptdf, base, classes, profs, sizes, placed, pooled, hits, later, part, parts, last, lasts,
    local_sem, ready, prof_send, prof_recv, size_send, size_recv, part_send, part_recv, last_send, last_recv,
):
    z, b = lax.axis_index("branch"), lax.axis_index("bus")
    members = n_branch * n_bus
    owners, scens, rows = base.shape
    half_blocks = ptdf.shape[0] // 256
    sites = profs.shape[-1]
    slots = sites // 128
    top = n_branch - 1
    mate = 1 - b

    def slot(level, core):
        return core * n_branch + level

    me = slot(z, b)
    upper = z // ((n_branch + 1) // 2)

    def at_least(left, right):
        return (left - right + 2 * n_branch) // (2 * n_branch)

    def farthest(i):
        k = top - i
        return upper * (i + at_least(i, z)) + (1 - upper) * (k - at_least(z, k))

    near = [farthest(top - 1 - i) for i in range(top)]

    def device(level, core):
        return {"branch": level, "bus": core}

    loads = [
        pltpu.make_async_copy(profile_hbm.at[0, 0, 0], profs.at[me], local_sem.at[0]),
        pltpu.make_async_copy(size_hbm.at[0, 0], sizes.at[me], local_sem.at[1]),
        pltpu.make_async_copy(block_hbm, block_ref, local_sem.at[6]),
        pltpu.make_async_copy(limit_hbm, limit_ref, local_sem.at[5]),
        pltpu.make_async_copy(class_hbm, classes, local_sem.at[2]),
        pltpu.make_async_copy(base_hbm.at[:, 0], base, local_sem.at[3]),
        pltpu.make_async_copy(ptdf_hbm, ptdf, local_sem.at[4]),
    ]
    loads[0].start()
    loads[1].start()

    barrier = pltpu.get_barrier_semaphore()
    for side in (-1, 1):
        level = z + side

        @pl.when((level >= 0) & (level < n_branch))
        def _():
            for core in (b, mate):
                pl.semaphore_signal(barrier, inc=1, device_id=device(level, core), device_id_type=MESH)

    pl.semaphore_signal(barrier, inc=1, device_id=device(z, mate), device_id_type=MESH)
    for load in loads[2:]:
        load.start()
    loads[0].wait()
    loads[1].wait()
    edges = jnp.where(z > 0, 1, 0) + jnp.where(z < top, 1, 0)
    pl.semaphore_wait(barrier, 1 + n_bus * edges)

    def remote(src, dst, send_sem, recv_sem, to):
        return pltpu.make_async_remote_copy(
            src_ref=src, dst_ref=dst, send_sem=send_sem, recv_sem=recv_sem,
            device_id=to, device_id_type=MESH,
        )

    def pass_on(index, to):
        remote(sizes.at[index], sizes.at[index], size_send, size_recv.at[index], to).start()
        remote(profs.at[index], profs.at[index], prof_send, prof_recv.at[index], to).start()

    def arrive(index):
        to = device(z, mate)
        remote(sizes.at[index], sizes.at[index], size_send, size_recv.at[index], to).wait_recv()
        remote(profs.at[index], profs.at[index], prof_send, prof_recv.at[index], to).wait_recv()

    def gap(level):
        return jnp.where(level > z, level - z, z - level)

    def announce(level):
        @pl.when(gap(level) > 1)
        def _():
            pl.semaphore_wait(ready.at[level], 1)

        onward = jnp.where(level > z, z - 1, z + 1)

        @pl.when((onward >= 0) & (onward < n_branch))
        def _():
            pl.semaphore_signal(ready.at[level], inc=1, device_id=device(onward, b), device_id_type=MESH)

    def offer(level):
        pass_on(me, device(level, b))

        @pl.when(gap(level) >= FAR)
        def _():
            pass_on(me, device(level, mate))

    for i, level in enumerate(near):
        announce(level)
        offer(level)
        if i == 0:
            pass_on(me, device(z, mate))

    for load in loads[2:5]:
        load.wait()
    class_row = classes[...].reshape(1, -1)
    rating = jnp.zeros(class_row.shape, jnp.float32)
    for c in range(limit_ref.shape[0]):
        rating = jnp.where(class_row == c, limit_ref[c], rating)
    inverse = 1.0 / rating
    line = lax.broadcasted_iota(jnp.int32, (members, 128), 0)
    for k in range(slots):
        number = jnp.zeros((members, 128), jnp.int32)
        for h in range(n_bus):
            for o in range(owners):
                number = jnp.where(line == slot(o, h), block_ref[0, k, h, o], number)
        for p in range(half_blocks):
            hits[p, k] = jnp.where(number == p, 1.0, 0.0)

    def place(level, core):
        index = slot(level, core)
        profile = profs[index].astype(jnp.float32)
        size = sizes[index]
        for p in range(half_blocks):
            total = weight = None
            for k in range(slots):
                hit = jnp.where(block_ref[0, k, core, level] == p, 1.0, 0.0)
                cut = slice(k * 128, (k + 1) * 128)
                term, own = profile[:, cut] * hit, size[:, cut] * hit
                total = term if total is None else total + term
                weight = own if weight is None else weight + own
            at = core * half_blocks + p
            placed[at, level] = total
            pooled[at, level] = (total * weight).astype(jnp.bfloat16)

    place(z, b)
    loads[5].wait()
    loads[6].wait()
    arrive(slot(z, mate))
    place(z, mate)
    for i, level in enumerate(near):
        index = slot(level, b)
        arrive(index)

        @pl.when(gap(level) < FAR)
        def _():
            pass_on(index, device(z, mate))

        place(level, b)
        if i > 0:
            arrive(slot(near[i - 1], mate))
            place(near[i - 1], mate)
    arrive(slot(near[-1], mate))
    place(near[-1], mate)

    def others():
        for i in range(top):
            level = farthest(i)
            for core in (b, mate):
                yield slot(level, core), device(level, core)
        yield slot(z, mate), device(z, mate)

    def all_but_one(ref, send_sem, recv_sem):
        return remote(
            ref.at[pl.ds(0, members - 1)], ref.at[pl.ds(0, members - 1)], send_sem, recv_sem, device(z, mate)
        )

    def sweep(final):
        count = owners * scens
        injected = jnp.concatenate(
            [pooled[i].reshape(count, 128) for i in range(2 * half_blocks)], axis=1
        )
        flow = jnp.dot(injected, ptdf[...], preferred_element_type=jnp.float32)
        flow = flow + base[...].reshape(flow.shape).astype(jnp.float32)
        if final:
            flow_out[...] = flow.astype(jnp.bfloat16).reshape(flow_out.shape)
        load = flow * inverse
        adjoint = ((1.0 + jnp.tanh(0.5 * (load * load - 1.0))) * load * inverse).astype(jnp.bfloat16)
        found = []
        for q in range(half_blocks):
            pair = lax.dot_general(
                adjoint, ptdf[q * 256:(q + 1) * 256, :], (((1,), (1,)), ((), ())),
                preferred_element_type=jnp.float32,
            )
            for i in range(2):
                product = pair[:, i * 128:(i + 1) * 128].reshape(owners, scens, 128) * placed[2 * q + i]
                found.append(jnp.sum(product, axis=1))
        full = [jnp.concatenate([found[p], found[half_blocks + p]], axis=0) for p in range(half_blocks)]
        values = []
        for k in range(slots):
            value = full[0] * hits[0, k]
            for p in range(1, half_blocks):
                value = value + full[p] * hits[p, k]
            values.append(value * (1.0 / scens))
        return jnp.concatenate(values, axis=1)

    parts[me] = sweep(False).astype(jnp.bfloat16)
    for _, to in others():
        remote(parts.at[me], parts.at[me], part_send, part_recv, to).start()
    all_but_one(parts, part_send, part_recv).wait_recv()
    gradient = jnp.sum(parts[...].astype(jnp.float32), axis=0)
    current = sizes[...].reshape(members, sites) + step_length * (1.0 - gradient)
    later[...] = current
    for p in range(half_blocks):
        weight = current[:, :128] * hits[p, 0]
        for k in range(1, slots):
            weight = weight + current[:, k * 128:(k + 1) * 128] * hits[p, k]
        for h in range(2):
            for o in range(owners):
                at = h * half_blocks + p
                r = slot(o, h)
                pooled[at, o] = (placed[at, o] * weight[r:r + 1]).astype(jnp.bfloat16)
    last[...] = sweep(True).reshape(last.shape)
    for to, where in others():
        remote(last.at[to], lasts.at[me], last_send, last_recv, where).start()
    lasts[me] = last[me]
    all_but_one(parts, part_send, part_recv).wait_send()
    all_but_one(profs, prof_send, prof_recv.at[0]).wait_send()
    all_but_one(sizes, size_send, size_recv.at[0]).wait_send()
    all_but_one(lasts, last_send, last_recv).wait_recv()
    total = jnp.sum(lasts[...], axis=0)
    size_out[...] = (later[pl.ds(me, 1), :] + step_length * (1.0 - total)).reshape(size_out.shape)
    all_but_one(lasts, last_send, last_recv).wait_send()


def per_device(n_branch, n_bus, ptdf, base_flow, rate_class, class_limit, site_block, profile, size_init):
    members = n_branch * n_bus
    owners, _, scens, rows = base_flow.shape
    pool = ptdf.shape[0]
    sites = profile.shape[-1]
    any_spec = pl.BlockSpec(memory_space=pl.ANY)
    blocks = jnp.transpose(site_block, (1, 3, 2, 0))
    vmem = pl.BlockSpec(memory_space=pltpu.VMEM)
    dma = pltpu.SemaphoreType.DMA
    return pl.pallas_call(
        functools.partial(kernel, n_branch, n_bus),
        out_shape=(
            pltpu.VMEM(size_init.shape, jnp.float32),
            pltpu.VMEM(base_flow.shape, jnp.bfloat16),
        ),
        in_specs=[any_spec] * 7,
        out_specs=(vmem, vmem),
        scratch_shapes=[
            pltpu.SMEM(class_limit.shape, jnp.float32),
            pltpu.SMEM(blocks.shape, jnp.int32),
            pltpu.VMEM(ptdf.shape, jnp.bfloat16),
            pltpu.VMEM((owners, scens, rows), jnp.bfloat16),
            pltpu.VMEM(rate_class.shape, jnp.int32),
            pltpu.VMEM((members, scens, sites), jnp.bfloat16),
            pltpu.VMEM((members, 1, sites), jnp.float32),
            pltpu.VMEM((pool // 128, owners, scens, 128), jnp.float32),
            pltpu.VMEM((pool // 128, owners, scens, 128), jnp.bfloat16),
            pltpu.VMEM((pool // 256, sites // 128, members, 128), jnp.float32),
            pltpu.VMEM((members, sites), jnp.float32),
            pltpu.VMEM((members, sites), jnp.float32),
            pltpu.VMEM((members, members, sites), jnp.bfloat16),
            pltpu.VMEM((members, 1, sites), jnp.float32),
            pltpu.VMEM((members, 1, sites), jnp.float32),
            dma((7,)), pltpu.SemaphoreType.REGULAR((n_branch,)),
            dma, dma((members,)), dma, dma((members,)),
            dma, dma, dma, dma,
        ],
        compiler_params=pltpu.CompilerParams(collective_id=0, has_side_effects=True),
        name="hosting",
    )(ptdf, base_flow, rate_class, class_limit, blocks, profile, size_init)


def solution(mesh):
    in_specs = (
        P(None, ("branch", "bus")),
        P("study", "scen", None, ("branch", "bus")),
        P(("branch", "bus")),
        P(),
        P("study", "scen", None, None),
        P(("study", "branch"), "scen", "bus", None, None),
        P(("study", "branch"), "scen", "bus", None),
    )
    out_specs = (
        P(("study", "branch"), "scen", "bus", None),
        P("study", "scen", None, ("branch", "bus")),
    )
    body = functools.partial(per_device, mesh.shape["branch"], mesh.shape["bus"])
    return jax.shard_map(body, mesh=mesh, in_specs=in_specs, out_specs=out_specs, check_vma=False)
```

```python
import functools
import jax
import jax.numpy as jnp
from jax import lax
from jax.experimental import pallas as pl
from jax.experimental.pallas import tpu as pltpu
from jax.sharding import PartitionSpec as P

step_length = 3.0
GROUP = ("branch", "bus")
MESH = pl.DeviceIdType.MESH


def kernel(
    n_branch, n_bus,
    ptdf_hbm, base_hbm, class_hbm, limit_hbm, block_hbm, profile_hbm, size_hbm,
    size_out, flow_out,
    limit_ref, block_ref, ptdf, base, classes, profs, sizes, later, pooled, sens, part, parts, last, lasts,
    local_sem, prof_send, prof_recv, size_send, size_recv, part_send, part_recv, last_send, last_recv,
):
    z, b = lax.axis_index("branch"), lax.axis_index("bus")
    members = n_branch * n_bus
    me = z * n_bus + b
    owners, scens, _ = base.shape
    pool = ptdf.shape[0]
    half_blocks = pool // 256
    sites = profs.shape[-1]
    slots = sites // 128

    partner = {"bus": lax.rem(b + 1, n_bus)}
    top = n_branch - 1

    def at_least(left, right):
        return (left - right + 2 * n_branch) // (2 * n_branch)

    def at(level, core):
        return level * n_bus + core

    def device(index):
        return {"branch": index // n_bus, "bus": lax.rem(index, n_bus)}

    def ahead(t):
        return lax.rem(me + t, members)

    def behind(t):
        return lax.rem(me - t + members, members)

    barrier = pltpu.get_barrier_semaphore()
    for t in range(1, members):
        pl.semaphore_signal(barrier, inc=1, device_id=device(ahead(t)), device_id_type=MESH)
    loads = [
        pltpu.make_async_copy(profile_hbm.at[0, 0, 0], profs.at[me], local_sem.at[0]),
        pltpu.make_async_copy(size_hbm.at[0, 0], sizes.at[me], local_sem.at[1]),
        pltpu.make_async_copy(class_hbm, classes, local_sem.at[2]),
        pltpu.make_async_copy(base_hbm.at[:, 0], base, local_sem.at[3]),
        pltpu.make_async_copy(ptdf_hbm, ptdf, local_sem.at[4]),
        pltpu.make_async_copy(limit_hbm, limit_ref, local_sem.at[5]),
        pltpu.make_async_copy(block_hbm, block_ref, local_sem.at[6]),
    ]
    for load in loads:
        load.start()
    loads[0].wait()
    loads[1].wait()
    pl.semaphore_wait(barrier, members - 1)

    def send(src, dst, send_sem, recv_sem, index):
        copy = pltpu.make_async_remote_copy(
            src_ref=src, dst_ref=dst, send_sem=send_sem, recv_sem=recv_sem,
            device_id=device(index), device_id_type=MESH,
        )
        copy.start()
        return copy

    def receive(dst, send_sem, recv_sem, index):
        pltpu.make_async_remote_copy(
            src_ref=dst, dst_ref=dst, send_sem=send_sem, recv_sem=recv_sem,
            device_id=device(index), device_id_type=MESH,
        ).wait_recv()

    mate = z * n_bus + lax.rem(b + 1, n_bus)
    sent = []

    def pass_on(t, index, to):
        sent.append(send(sizes.at[index], sizes.at[index], size_send, size_recv.at[index], to))
        sent.append(send(profs.at[index], profs.at[index], prof_send, prof_recv.at[index], to))

    def arrive(index):
        receive(sizes.at[index], size_send, size_recv.at[index], mate)
        receive(profs.at[index], prof_send, prof_recv.at[index], mate)

    for t in range(1, n_branch):
        pass_on(t, me, lax.rem(z + t, n_branch) * n_bus + b)
    pass_on(0, me, mate)

    loads[2].wait()
    loads[5].wait()
    loads[6].wait()
    class_row = classes[...].reshape(1, -1)
    rating = jnp.zeros(class_row.shape, jnp.float32)
    for c in range(limit_ref.shape[0]):
        rating = jnp.where(class_row == c, limit_ref[c], rating)
    inverse = 1.0 / rating
    loads[3].wait()
    loads[4].wait()

    for t in range(1, n_branch):
        index = lax.rem(z - t + n_branch, n_branch) * n_bus + b
        arrive(index)
        pass_on(n_branch - 1 + t, index, mate)
    for t in range(n_branch):
        arrive(lax.rem(z - t + n_branch, n_branch) * n_bus + lax.rem(b + 1, n_bus))

    def remote(src, dst, send_sem, recv_sem, device):
        return pltpu.make_async_remote_copy(
            src_ref=src, dst_ref=dst, send_sem=send_sem, recv_sem=recv_sem,
            device_id=device, device_id_type=MESH,
        )

    upper = z // ((n_branch + 1) // 2)

    def others():
        for i in range(top):
            k = top - i
            level = upper * (i + at_least(i, z)) + (1 - upper) * (k - at_least(z, k))
            for c in range(n_bus):
                yield at(level, lax.rem(b + c, n_bus)), {"branch": level, "bus": lax.rem(b + c, n_bus)}
        yield at(z, lax.rem(b + 1, n_bus)), partner

    def all_but_one(ref, send_sem, recv_sem):
        return remote(ref.at[pl.ds(0, members - 1)], ref.at[pl.ds(0, members - 1)], send_sem, recv_sem, partner)

    def sweep(final):
        current = later if final else sizes
        for o in range(owners):
            for h in range(2):
                j = 2 * o + h
                injected = (current[j] * profs[j].astype(jnp.float32)).astype(jnp.bfloat16).astype(jnp.float32)
                for p in range(half_blocks):
                    total = None
                    for k in range(slots):
                        hit = jnp.where(block_ref[0, k, h, o] == p, 1.0, 0.0)
                        term = injected[:, k * 128:(k + 1) * 128] * hit
                        total = term if total is None else total + term
                    at = (h * half_blocks + p) * 128
                    pooled[o * scens:(o + 1) * scens, at:at + 128] = total.astype(jnp.bfloat16)
        flow = jnp.dot(pooled[...], ptdf[...], preferred_element_type=jnp.float32)
        flow = flow + base[...].reshape(flow.shape).astype(jnp.float32)
        if final:
            flow_out[...] = flow.astype(jnp.bfloat16).reshape(flow_out.shape)
        load = flow * inverse
        adjoint = ((1.0 + jnp.tanh(0.5 * (load * load - 1.0))) * load * inverse).astype(jnp.bfloat16)
        for q in range(half_blocks):
            pair = lax.dot_general(
                adjoint, ptdf[q * 256:(q + 1) * 256, :], (((1,), (1,)), ((), ())),
                preferred_element_type=jnp.float32,
            )
            sens[2 * q] = pair[:, :128]
            sens[2 * q + 1] = pair[:, 128:]
        for o in range(owners):
            for h in range(2):
                j = 2 * o + h
                for k in range(slots):
                    rows = sens[h * half_blocks + block_ref[0, k, h, o], o * scens:(o + 1) * scens, :]
                    cut = slice(k * 128, (k + 1) * 128)
                    value = jnp.sum(rows * profs[j, :, cut].astype(jnp.float32), axis=0, keepdims=True) * (1.0 / scens)
                    if final:
                        last[j, :, cut] = value
                    else:
                        part[j:j + 1, cut] = value

    sweep(False)
    parts[me] = part[...].astype(jnp.bfloat16)
    for _, device in others():
        remote(parts.at[me], parts.at[me], part_send, part_recv, device).start()
    all_but_one(parts, part_send, part_recv).wait_recv()
    gradient = jnp.sum(parts[...].astype(jnp.float32), axis=0)
    for j in range(members):
        later[j] = sizes[j] + step_length * (1.0 - gradient[j:j + 1, :])
    sweep(True)
    for to, device in others():
        remote(last.at[to], lasts.at[me], last_send, last_recv, device).start()
    lasts[me] = last[me]
    all_but_one(parts, part_send, part_recv).wait_send()
    all_but_one(profs, prof_send, prof_recv.at[0]).wait_send()
    all_but_one(sizes, size_send, size_recv.at[0]).wait_send()
    all_but_one(lasts, last_send, last_recv).wait_recv()
    total = jnp.sum(lasts[...], axis=0)
    size_out[...] = (later[me] + step_length * (1.0 - total)).reshape(size_out.shape)
    all_but_one(lasts, last_send, last_recv).wait_send()


def writer(size_ref, flow_ref, size_hbm, flow_hbm, sems):
    copies = [
        pltpu.make_async_copy(flow_ref, flow_hbm, sems.at[0]),
        pltpu.make_async_copy(size_ref, size_hbm, sems.at[1]),
    ]
    for copy in copies:
        copy.start()
    for copy in copies:
        copy.wait()


def per_device(n_branch, n_bus, ptdf, base_flow, rate_class, class_limit, site_block, profile, size_init):
    members = n_branch * n_bus
    owners, _, scens, rows = base_flow.shape
    pool = ptdf.shape[0]
    sites = profile.shape[-1]
    any_spec = pl.BlockSpec(memory_space=pl.ANY)
    blocks = jnp.transpose(site_block, (1, 3, 2, 0))
    vmem = pl.BlockSpec(memory_space=pltpu.VMEM)
    dma = pltpu.SemaphoreType.DMA
    size, flow = pl.pallas_call(
        functools.partial(kernel, n_branch, n_bus),
        out_shape=(
            pltpu.VMEM(size_init.shape, jnp.float32),
            pltpu.VMEM(base_flow.shape, jnp.bfloat16),
        ),
        in_specs=[any_spec] * 7,
        out_specs=(vmem, vmem),
        scratch_shapes=[
            pltpu.SMEM(class_limit.shape, jnp.float32),
            pltpu.SMEM(blocks.shape, jnp.int32),
            pltpu.VMEM(ptdf.shape, jnp.bfloat16),
            pltpu.VMEM((owners, scens, rows), jnp.bfloat16),
            pltpu.VMEM(rate_class.shape, jnp.int32),
            pltpu.VMEM((members, scens, sites), jnp.bfloat16),
            pltpu.VMEM((members, 1, sites), jnp.float32),
            pltpu.VMEM((members, 1, sites), jnp.float32),
            pltpu.VMEM((owners * scens, pool), jnp.bfloat16),
            pltpu.VMEM((pool // 128, owners * scens, 128), jnp.float32),
            pltpu.VMEM((members, sites), jnp.float32),
            pltpu.VMEM((members, members, sites), jnp.bfloat16),
            pltpu.VMEM((members, 1, sites), jnp.float32),
            pltpu.VMEM((members, 1, sites), jnp.float32),
            dma((7,)),
            dma, dma((members,)), dma, dma((members,)),
            dma, dma, dma, dma,
        ],
        compiler_params=pltpu.CompilerParams(collective_id=0, has_side_effects=True),
        name="hosting",
    )(ptdf, base_flow, rate_class, class_limit, blocks, profile, size_init)
    size, flow = [pltpu.with_memory_space_constraint(v, pltpu.VMEM) for v in (size, flow)]
    return pl.pallas_call(
        writer,
        out_shape=(
            jax.ShapeDtypeStruct(size_init.shape, jnp.float32),
            jax.ShapeDtypeStruct(base_flow.shape, jnp.bfloat16),
        ),
        in_specs=[any_spec, any_spec],
        out_specs=(any_spec, any_spec),
        scratch_shapes=[dma((2,))],
        name="writer",
    )(size, flow)


def solution(mesh):
    in_specs = (
        P(None, ("branch", "bus")),
        P("study", "scen", None, ("branch", "bus")),
        P(("branch", "bus")),
        P(),
        P("study", "scen", None, None),
        P(("study", "branch"), "scen", "bus", None, None),
        P(("study", "branch"), "scen", "bus", None),
    )
    out_specs = (
        P(("study", "branch"), "scen", "bus", None),
        P("study", "scen", None, ("branch", "bus")),
    )
    body = functools.partial(per_device, mesh.shape["branch"], mesh.shape["bus"])
    return jax.shard_map(body, mesh=mesh, in_specs=in_specs, out_specs=out_specs, check_vma=False)
```

```python
import functools
import jax
import jax.numpy as jnp
from jax import lax
from jax.experimental import pallas as pl
from jax.experimental.pallas import tpu as pltpu
from jax.sharding import PartitionSpec as P

step_length = 3.0
MESH = pl.DeviceIdType.MESH


def kernel(
    n_branch, n_bus,
    ptdf_hbm, base_hbm, class_hbm, limit_hbm, block_hbm, profile_hbm, size_hbm,
    size_out, flow_out,
    limit_ref, block_ref, ptdf, base, classes, profs, sizes, placed, pooled, hits, weights, partial, later, parts, last, lasts,
    local_sem, prof_send, prof_recv, size_send, size_recv, part_send, part_recv, last_send, last_recv,
):
    z, b = lax.axis_index("branch"), lax.axis_index("bus")
    members = n_branch * n_bus
    owners, scens, rows = base.shape
    half_blocks = ptdf.shape[0] // 256
    sites = profs.shape[-1]
    slots = sites // 128
    top = n_branch - 1
    mate = 1 - b

    def slot(level, core):
        return core * n_branch + level

    me = slot(z, b)
    upper = z // ((n_branch + 1) // 2)

    def at_least(left, right):
        return (left - right + 2 * n_branch) // (2 * n_branch)

    def farthest(i):
        k = top - i
        return upper * (i + at_least(i, z)) + (1 - upper) * (k - at_least(z, k))

    near = [farthest(top - 1 - i) for i in range(top)]

    def device(level, core):
        return {"branch": level, "bus": core}

    loads = [
        pltpu.make_async_copy(profile_hbm.at[0, 0, 0], profs.at[me], local_sem.at[0]),
        pltpu.make_async_copy(size_hbm.at[0, 0], sizes.at[me], local_sem.at[1]),
        pltpu.make_async_copy(block_hbm, block_ref, local_sem.at[6]),
        pltpu.make_async_copy(limit_hbm, limit_ref, local_sem.at[5]),
        pltpu.make_async_copy(class_hbm, classes, local_sem.at[2]),
        pltpu.make_async_copy(base_hbm.at[:, 0], base, local_sem.at[3]),
        pltpu.make_async_copy(ptdf_hbm, ptdf, local_sem.at[4]),
    ]
    loads[0].start()
    loads[1].start()

    barrier = pltpu.get_barrier_semaphore()
    for i in range(top):
        level = farthest(i)
        for core in (b, mate):
            pl.semaphore_signal(barrier, inc=1, device_id=device(level, core), device_id_type=MESH)
    pl.semaphore_signal(barrier, inc=1, device_id=device(z, mate), device_id_type=MESH)
    for load in loads[2:]:
        load.start()
    loads[0].wait()
    loads[1].wait()
    pl.semaphore_wait(barrier, members - 1)

    def remote(src, dst, send_sem, recv_sem, to):
        return pltpu.make_async_remote_copy(
            src_ref=src, dst_ref=dst, send_sem=send_sem, recv_sem=recv_sem,
            device_id=to, device_id_type=MESH,
        )

    def pass_on(index, to):
        remote(profs.at[index], profs.at[index], prof_send, prof_recv.at[index], to).start()

    def arrive(index):
        remote(profs.at[index], profs.at[index], prof_send, prof_recv.at[index], device(z, mate)).wait_recv()

    for level in near[::-1]:
        pass_on(me, device(level, b))
    for level in near[::-1]:
        for core in (b, mate):
            remote(sizes.at[me], sizes.at[me], size_send, size_recv, device(level, core)).start()
    remote(sizes.at[me], sizes.at[me], size_send, size_recv, device(z, mate)).start()
    pass_on(me, device(z, mate))

    for load in loads[2:5]:
        load.wait()
    class_row = classes[...].reshape(1, -1)
    rating = jnp.zeros(class_row.shape, jnp.float32)
    for c in range(limit_ref.shape[0]):
        rating = jnp.where(class_row == c, limit_ref[c], rating)
    inverse = 1.0 / rating
    line = lax.broadcasted_iota(jnp.int32, (members, 128), 0)
    for k in range(slots):
        number = jnp.zeros((members, 128), jnp.int32)
        for h in range(n_bus):
            for o in range(owners):
                number = jnp.where(line == slot(o, h), block_ref[0, k, h, o], number)
        for p in range(half_blocks):
            hits[p, k] = jnp.where(number == p, 1.0, 0.0)

    def all_but_one(ref, send_sem, recv_sem):
        return remote(
            ref.at[pl.ds(0, members - 1)], ref.at[pl.ds(0, members - 1)], send_sem, recv_sem, device(z, mate)
        )

    def place(level, core):
        profile = profs[slot(level, core)].astype(jnp.float32)
        for p in range(half_blocks):
            total = None
            for k in range(slots):
                term = profile[:, k * 128:(k + 1) * 128] * jnp.where(block_ref[0, k, core, level] == p, 1.0, 0.0)
                total = term if total is None else total + term
            placed[core * half_blocks + p, level] = total

    def weigh(level, core):
        for p in range(half_blocks):
            at = core * half_blocks + p
            weight = weights[p, pl.ds(slot(level, core), 1), :]
            pooled[at, level] = (placed[at, level] * weight).astype(jnp.bfloat16)

    def spread(current):
        for p in range(half_blocks):
            weight = current[:, :128] * hits[p, 0]
            for k in range(1, slots):
                weight = weight + current[:, k * 128:(k + 1) * 128] * hits[p, k]
            weights[p] = weight

    def half_flow(core):
        count = owners * scens
        injected = jnp.concatenate(
            [pooled[core * half_blocks + i].reshape(count, 128) for i in range(half_blocks)], axis=1
        )
        depth = half_blocks * 128
        used = ptdf[pl.ds(pl.multiple_of(core * depth, depth), depth), :]
        return jnp.dot(injected, used, preferred_element_type=jnp.float32)

    place(z, b)
    for level in near:
        arrive(slot(level, b))
        pass_on(slot(level, b), device(z, mate))
        place(level, b)
    all_but_one(sizes, size_send, size_recv).wait_recv()
    spread(sizes[...].reshape(members, sites))
    for level in [z] + near:
        weigh(level, b)
    loads[5].wait()
    loads[6].wait()
    half = half_flow(b)
    partial[...] = half + base[...].reshape(half.shape).astype(jnp.float32)
    for level in [z] + near:
        arrive(slot(level, mate))
        place(level, mate)
        weigh(level, mate)

    def others():
        for i in range(top):
            level = farthest(i)
            for core in (b, mate):
                yield slot(level, core), device(level, core)
        yield slot(z, mate), device(z, mate)

    def sweep(final):
        if final:
            count = owners * scens
            injected = jnp.concatenate(
                [pooled[i].reshape(count, 128) for i in range(2 * half_blocks)], axis=1
            )
            flow = jnp.dot(injected, ptdf[...], preferred_element_type=jnp.float32)
            flow = flow + base[...].reshape(flow.shape).astype(jnp.float32)
        else:
            flow = partial[...] + half_flow(mate)
        if final:
            flow_out[...] = flow.astype(jnp.bfloat16).reshape(flow_out.shape)
        load = flow * inverse
        adjoint = ((1.0 + jnp.tanh(0.5 * (load * load - 1.0))) * load * inverse).astype(jnp.bfloat16)
        found = []
        for q in range(half_blocks):
            pair = lax.dot_general(
                adjoint, ptdf[q * 256:(q + 1) * 256, :], (((1,), (1,)), ((), ())),
                preferred_element_type=jnp.float32,
            )
            for i in range(2):
                product = pair[:, i * 128:(i + 1) * 128].reshape(owners, scens, 128) * placed[2 * q + i]
                found.append(jnp.sum(product, axis=1))
        full = [jnp.concatenate([found[p], found[half_blocks + p]], axis=0) for p in range(half_blocks)]
        values = []
        for k in range(slots):
            value = full[0] * hits[0, k]
            for p in range(1, half_blocks):
                value = value + full[p] * hits[p, k]
            values.append(value * (1.0 / scens))
        return jnp.concatenate(values, axis=1)

    parts[me] = sweep(False).astype(jnp.bfloat16)
    for _, to in others():
        remote(parts.at[me], parts.at[me], part_send, part_recv, to).start()
    all_but_one(parts, part_send, part_recv).wait_recv()
    gradient = jnp.sum(parts[...].astype(jnp.float32), axis=0)
    current = sizes[...].reshape(members, sites) + step_length * (1.0 - gradient)
    later[...] = current
    for p in range(half_blocks):
        weight = current[:, :128] * hits[p, 0]
        for k in range(1, slots):
            weight = weight + current[:, k * 128:(k + 1) * 128] * hits[p, k]
        for h in range(2):
            for o in range(owners):
                at = h * half_blocks + p
                r = slot(o, h)
                pooled[at, o] = (placed[at, o] * weight[r:r + 1]).astype(jnp.bfloat16)
    last[...] = sweep(True).reshape(last.shape)
    for to, where in others():
        remote(last.at[to], lasts.at[me], last_send, last_recv, where).start()
    lasts[me] = last[me]
    all_but_one(parts, part_send, part_recv).wait_send()
    all_but_one(profs, prof_send, prof_recv.at[0]).wait_send()
    all_but_one(sizes, size_send, size_recv).wait_send()
    all_but_one(lasts, last_send, last_recv).wait_recv()
    total = jnp.sum(lasts[...], axis=0)
    size_out[...] = (later[pl.ds(me, 1), :] + step_length * (1.0 - total)).reshape(size_out.shape)
    all_but_one(lasts, last_send, last_recv).wait_send()


def writer(size_ref, flow_ref, size_hbm, flow_hbm, sems):
    copies = [
        pltpu.make_async_copy(flow_ref, flow_hbm, sems.at[0]),
        pltpu.make_async_copy(size_ref, size_hbm, sems.at[1]),
    ]
    for copy in copies:
        copy.start()
    for copy in copies:
        copy.wait()


def per_device(n_branch, n_bus, ptdf, base_flow, rate_class, class_limit, site_block, profile, size_init):
    members = n_branch * n_bus
    owners, _, scens, rows = base_flow.shape
    pool = ptdf.shape[0]
    sites = profile.shape[-1]
    any_spec = pl.BlockSpec(memory_space=pl.ANY)
    blocks = jnp.transpose(site_block, (1, 3, 2, 0))
    vmem = pl.BlockSpec(memory_space=pltpu.VMEM)
    dma = pltpu.SemaphoreType.DMA
    size, flow = pl.pallas_call(
        functools.partial(kernel, n_branch, n_bus),
        out_shape=(
            pltpu.VMEM(size_init.shape, jnp.float32),
            pltpu.VMEM(base_flow.shape, jnp.bfloat16),
        ),
        in_specs=[any_spec] * 7,
        out_specs=(vmem, vmem),
        scratch_shapes=[
            pltpu.SMEM(class_limit.shape, jnp.float32),
            pltpu.SMEM(blocks.shape, jnp.int32),
            pltpu.VMEM(ptdf.shape, jnp.bfloat16),
            pltpu.VMEM((owners, scens, rows), jnp.bfloat16),
            pltpu.VMEM(rate_class.shape, jnp.int32),
            pltpu.VMEM((members, scens, sites), jnp.bfloat16),
            pltpu.VMEM((members, 1, sites), jnp.float32),
            pltpu.VMEM((pool // 128, owners, scens, 128), jnp.float32),
            pltpu.VMEM((pool // 128, owners, scens, 128), jnp.bfloat16),
            pltpu.VMEM((pool // 256, sites // 128, members, 128), jnp.float32),
            pltpu.VMEM((pool // 256, members, 128), jnp.float32),
            pltpu.VMEM((owners * scens, rows), jnp.float32),
            pltpu.VMEM((members, sites), jnp.float32),
            pltpu.VMEM((members, members, sites), jnp.bfloat16),
            pltpu.VMEM((members, 1, sites), jnp.float32),
            pltpu.VMEM((members, 1, sites), jnp.float32),
            dma((7,)),
            dma, dma((members,)), dma, dma,
            dma, dma, dma, dma,
        ],
        compiler_params=pltpu.CompilerParams(collective_id=0, has_side_effects=True),
        name="hosting",
    )(ptdf, base_flow, rate_class, class_limit, blocks, profile, size_init)
    size, flow = [pltpu.with_memory_space_constraint(v, pltpu.VMEM) for v in (size, flow)]
    return pl.pallas_call(
        writer,
        out_shape=(
            jax.ShapeDtypeStruct(size_init.shape, jnp.float32),
            jax.ShapeDtypeStruct(base_flow.shape, jnp.bfloat16),
        ),
        in_specs=[any_spec, any_spec],
        out_specs=(any_spec, any_spec),
        scratch_shapes=[dma((2,))],
        name="writer",
    )(size, flow)


def solution(mesh):
    in_specs = (
        P(None, ("branch", "bus")),
        P("study", "scen", None, ("branch", "bus")),
        P(("branch", "bus")),
        P(),
        P("study", "scen", None, None),
        P(("study", "branch"), "scen", "bus", None, None),
        P(("study", "branch"), "scen", "bus", None),
    )
    out_specs = (
        P(("study", "branch"), "scen", "bus", None),
        P("study", "scen", None, ("branch", "bus")),
    )
    body = functools.partial(per_device, mesh.shape["branch"], mesh.shape["bus"])
    return jax.shard_map(body, mesh=mesh, in_specs=in_specs, out_specs=out_specs, check_vma=False)
```

```python
import functools
import jax
import jax.numpy as jnp
from jax import lax
from jax.experimental import pallas as pl
from jax.experimental.pallas import tpu as pltpu
from jax.sharding import PartitionSpec as P

step_length = 3.0
MESH = pl.DeviceIdType.MESH


def kernel(
    n_branch, n_bus,
    ptdf_hbm, base_hbm, class_hbm, limit_hbm, block_hbm, profile_hbm, size_hbm,
    size_out, flow_out,
    limit_ref, block_ref, ptdf, base, classes, profs, sizes, placed, pooled, hits, weights, partial, later, parts, last, lasts,
    local_sem, prof_send, prof_recv, size_send, size_recv, part_send, part_recv, last_send, last_recv,
):
    z, b = lax.axis_index("branch"), lax.axis_index("bus")
    members = n_branch * n_bus
    owners, scens, rows = base.shape
    half_blocks = ptdf.shape[0] // 256
    sites = profs.shape[-1]
    slots = sites // 128
    top = n_branch - 1
    mate = 1 - b

    def slot(level, core):
        return core * n_branch + level

    me = slot(z, b)
    upper = z // ((n_branch + 1) // 2)

    def at_least(left, right):
        return (left - right + 2 * n_branch) // (2 * n_branch)

    def farthest(i):
        k = top - i
        return upper * (i + at_least(i, z)) + (1 - upper) * (k - at_least(z, k))

    near = [farthest(top - 1 - i) for i in range(top)]

    def device(level, core):
        return {"branch": level, "bus": core}

    loads = [
        pltpu.make_async_copy(profile_hbm.at[0, 0, 0], profs.at[me], local_sem.at[0]),
        pltpu.make_async_copy(size_hbm.at[0, 0], sizes.at[me], local_sem.at[1]),
        pltpu.make_async_copy(block_hbm, block_ref, local_sem.at[6]),
        pltpu.make_async_copy(limit_hbm, limit_ref, local_sem.at[5]),
        pltpu.make_async_copy(class_hbm, classes, local_sem.at[2]),
        pltpu.make_async_copy(base_hbm.at[:, 0], base, local_sem.at[3]),
        pltpu.make_async_copy(ptdf_hbm, ptdf, local_sem.at[4]),
    ]
    loads[0].start()
    loads[1].start()

    barrier = pltpu.get_barrier_semaphore()
    for i in range(top):
        level = farthest(i)
        for core in (b, mate):
            pl.semaphore_signal(barrier, inc=1, device_id=device(level, core), device_id_type=MESH)
    pl.semaphore_signal(barrier, inc=1, device_id=device(z, mate), device_id_type=MESH)
    for load in loads[2:]:
        load.start()
    loads[0].wait()
    loads[1].wait()
    pl.semaphore_wait(barrier, members - 1)

    def remote(src, dst, send_sem, recv_sem, to):
        return pltpu.make_async_remote_copy(
            src_ref=src, dst_ref=dst, send_sem=send_sem, recv_sem=recv_sem,
            device_id=to, device_id_type=MESH,
        )

    def pass_on(index, to):
        remote(profs.at[index], profs.at[index], prof_send, prof_recv.at[index], to).start()

    def arrive(index):
        remote(profs.at[index], profs.at[index], prof_send, prof_recv.at[index], device(z, mate)).wait_recv()

    for level in near[::-1]:
        pass_on(me, device(level, b))
    for level in near[::-1]:
        for core in (b, mate):
            remote(sizes.at[me], sizes.at[me], size_send, size_recv, device(level, core)).start()
    remote(sizes.at[me], sizes.at[me], size_send, size_recv, device(z, mate)).start()
    pass_on(me, device(z, mate))

    for load in loads[2:5]:
        load.wait()
    class_row = classes[...].reshape(1, -1)
    rating = jnp.zeros(class_row.shape, jnp.float32)
    for c in range(limit_ref.shape[0]):
        rating = jnp.where(class_row == c, limit_ref[c], rating)
    inverse = 1.0 / rating
    line = lax.broadcasted_iota(jnp.int32, (members, 128), 0)
    for k in range(slots):
        number = jnp.zeros((members, 128), jnp.int32)
        for h in range(n_bus):
            for o in range(owners):
                number = jnp.where(line == slot(o, h), block_ref[0, k, h, o], number)
        for p in range(half_blocks):
            hits[p, k] = jnp.where(number == p, 1.0, 0.0)

    def all_but_one(ref, send_sem, recv_sem):
        return remote(
            ref.at[pl.ds(0, members - 1)], ref.at[pl.ds(0, members - 1)], send_sem, recv_sem, device(z, mate)
        )

    def place(level, core):
        profile = profs[slot(level, core)].astype(jnp.float32)
        for p in range(half_blocks):
            total = None
            for k in range(slots):
                term = profile[:, k * 128:(k + 1) * 128] * jnp.where(block_ref[0, k, core, level] == p, 1.0, 0.0)
                total = term if total is None else total + term
            placed[core * half_blocks + p, level] = total

    def weigh(level, core):
        for p in range(half_blocks):
            at = core * half_blocks + p
            weight = weights[p, pl.ds(slot(level, core), 1), :]
            pooled[at, level] = (placed[at, level] * weight).astype(jnp.bfloat16)

    def spread(current):
        for p in range(half_blocks):
            weight = current[:, :128] * hits[p, 0]
            for k in range(1, slots):
                weight = weight + current[:, k * 128:(k + 1) * 128] * hits[p, k]
            weights[p] = weight

    def half_flow(core):
        count = owners * scens
        injected = jnp.concatenate(
            [pooled[core * half_blocks + i].reshape(count, 128) for i in range(half_blocks)], axis=1
        )
        depth = half_blocks * 128
        used = ptdf[pl.ds(pl.multiple_of(core * depth, depth), depth), :]
        return jnp.dot(injected, used, preferred_element_type=jnp.float32)

    place(z, b)
    for level in near:
        arrive(slot(level, b))
        pass_on(slot(level, b), device(z, mate))
        place(level, b)
    all_but_one(sizes, size_send, size_recv).wait_recv()
    spread(sizes[...].reshape(members, sites))
    for level in [z] + near:
        weigh(level, b)
    loads[5].wait()
    loads[6].wait()
    half = half_flow(b)
    partial[...] = half + base[...].reshape(half.shape).astype(jnp.float32)
    for level in [z] + near:
        arrive(slot(level, mate))
        place(level, mate)
        weigh(level, mate)

    def others():
        for i in range(top):
            level = farthest(i)
            for core in (b, mate):
                yield slot(level, core), device(level, core)
        yield slot(z, mate), device(z, mate)

    def sweep(final):
        if final:
            count = owners * scens
            injected = jnp.concatenate(
                [pooled[i].reshape(count, 128) for i in range(2 * half_blocks)], axis=1
            )
            flow = jnp.dot(injected, ptdf[...], preferred_element_type=jnp.float32)
            flow = flow + base[...].reshape(flow.shape).astype(jnp.float32)
        else:
            flow = partial[...] + half_flow(mate)
        if final:
            flow_out[...] = flow.astype(jnp.bfloat16).reshape(flow_out.shape)
        wide = rows // 2
        adjoints = []
        for c in range(2):
            side = slice(c * wide, (c + 1) * wide)
            load = flow[:, side] * inverse[:, side]
            adjoints.append(
                ((1.0 + jnp.tanh(0.5 * (load * load - 1.0))) * load * inverse[:, side]).astype(jnp.bfloat16)
            )
        found = []
        for q in range(half_blocks):
            pair = None
            for c in range(2):
                term = lax.dot_general(
                    adjoints[c], ptdf[q * 256:(q + 1) * 256, c * wide:(c + 1) * wide], (((1,), (1,)), ((), ())),
                    preferred_element_type=jnp.float32,
                )
                pair = term if pair is None else pair + term
            for i in range(2):
                product = pair[:, i * 128:(i + 1) * 128].reshape(owners, scens, 128) * placed[2 * q + i]
                found.append(jnp.sum(product, axis=1))
        full = [jnp.concatenate([found[p], found[half_blocks + p]], axis=0) for p in range(half_blocks)]
        values = []
        for k in range(slots):
            value = full[0] * hits[0, k]
            for p in range(1, half_blocks):
                value = value + full[p] * hits[p, k]
            values.append(value * (1.0 / scens))
        return jnp.concatenate(values, axis=1)

    parts[me] = sweep(False).astype(jnp.bfloat16)
    for _, to in others():
        remote(parts.at[me], parts.at[me], part_send, part_recv, to).start()
    all_but_one(parts, part_send, part_recv).wait_recv()
    gradient = jnp.sum(parts[...].astype(jnp.float32), axis=0)
    current = sizes[...].reshape(members, sites) + step_length * (1.0 - gradient)
    later[...] = current
    for p in range(half_blocks):
        weight = current[:, :128] * hits[p, 0]
        for k in range(1, slots):
            weight = weight + current[:, k * 128:(k + 1) * 128] * hits[p, k]
        for h in range(2):
            for o in range(owners):
                at = h * half_blocks + p
                r = slot(o, h)
                pooled[at, o] = (placed[at, o] * weight[r:r + 1]).astype(jnp.bfloat16)
    last[...] = sweep(True).reshape(last.shape)
    for to, where in others():
        remote(last.at[to], lasts.at[me], last_send, last_recv, where).start()
    lasts[me] = last[me]
    all_but_one(parts, part_send, part_recv).wait_send()
    all_but_one(profs, prof_send, prof_recv.at[0]).wait_send()
    all_but_one(sizes, size_send, size_recv).wait_send()
    all_but_one(lasts, last_send, last_recv).wait_recv()
    total = jnp.sum(lasts[...], axis=0)
    size_out[...] = (later[pl.ds(me, 1), :] + step_length * (1.0 - total)).reshape(size_out.shape)
    all_but_one(lasts, last_send, last_recv).wait_send()


def writer(size_ref, flow_ref, size_hbm, flow_hbm, sems):
    copies = [
        pltpu.make_async_copy(flow_ref, flow_hbm, sems.at[0]),
        pltpu.make_async_copy(size_ref, size_hbm, sems.at[1]),
    ]
    for copy in copies:
        copy.start()
    for copy in copies:
        copy.wait()


def per_device(n_branch, n_bus, ptdf, base_flow, rate_class, class_limit, site_block, profile, size_init):
    members = n_branch * n_bus
    owners, _, scens, rows = base_flow.shape
    pool = ptdf.shape[0]
    sites = profile.shape[-1]
    any_spec = pl.BlockSpec(memory_space=pl.ANY)
    blocks = jnp.transpose(site_block, (1, 3, 2, 0))
    vmem = pl.BlockSpec(memory_space=pltpu.VMEM)
    dma = pltpu.SemaphoreType.DMA
    size, flow = pl.pallas_call(
        functools.partial(kernel, n_branch, n_bus),
        out_shape=(
            pltpu.VMEM(size_init.shape, jnp.float32),
            pltpu.VMEM(base_flow.shape, jnp.bfloat16),
        ),
        in_specs=[any_spec] * 7,
        out_specs=(vmem, vmem),
        scratch_shapes=[
            pltpu.SMEM(class_limit.shape, jnp.float32),
            pltpu.SMEM(blocks.shape, jnp.int32),
            pltpu.VMEM(ptdf.shape, jnp.bfloat16),
            pltpu.VMEM((owners, scens, rows), jnp.bfloat16),
            pltpu.VMEM(rate_class.shape, jnp.int32),
            pltpu.VMEM((members, scens, sites), jnp.bfloat16),
            pltpu.VMEM((members, 1, sites), jnp.float32),
            pltpu.VMEM((pool // 128, owners, scens, 128), jnp.float32),
            pltpu.VMEM((pool // 128, owners, scens, 128), jnp.bfloat16),
            pltpu.VMEM((pool // 256, sites // 128, members, 128), jnp.float32),
            pltpu.VMEM((pool // 256, members, 128), jnp.float32),
            pltpu.VMEM((owners * scens, rows), jnp.float32),
            pltpu.VMEM((members, sites), jnp.float32),
            pltpu.VMEM((members, members, sites), jnp.bfloat16),
            pltpu.VMEM((members, 1, sites), jnp.float32),
            pltpu.VMEM((members, 1, sites), jnp.float32),
            dma((7,)),
            dma, dma((members,)), dma, dma,
            dma, dma, dma, dma,
        ],
        compiler_params=pltpu.CompilerParams(collective_id=0, has_side_effects=True),
        name="hosting",
    )(ptdf, base_flow, rate_class, class_limit, blocks, profile, size_init)
    size, flow = [pltpu.with_memory_space_constraint(v, pltpu.VMEM) for v in (size, flow)]
    return pl.pallas_call(
        writer,
        out_shape=(
            jax.ShapeDtypeStruct(size_init.shape, jnp.float32),
            jax.ShapeDtypeStruct(base_flow.shape, jnp.bfloat16),
        ),
        in_specs=[any_spec, any_spec],
        out_specs=(any_spec, any_spec),
        scratch_shapes=[dma((2,))],
        name="writer",
    )(size, flow)


def solution(mesh):
    in_specs = (
        P(None, ("branch", "bus")),
        P("study", "scen", None, ("branch", "bus")),
        P(("branch", "bus")),
        P(),
        P("study", "scen", None, None),
        P(("study", "branch"), "scen", "bus", None, None),
        P(("study", "branch"), "scen", "bus", None),
    )
    out_specs = (
        P(("study", "branch"), "scen", "bus", None),
        P("study", "scen", None, ("branch", "bus")),
    )
    body = functools.partial(per_device, mesh.shape["branch"], mesh.shape["bus"])
    return jax.shard_map(body, mesh=mesh, in_specs=in_specs, out_specs=out_specs, check_vma=False)
```
